32 devices in a mesh: ctx: 8 (over y, x, core), qry: 4 (over z).
Axes of the slice: x: 2, y: 2, z: 4, core: 2. Of those that a mesh axis runs over, the one named last changes fastest.
Arguments:
- hist_bins: int32 [512, 16], P(('ctx', 'qry')), may hold values from 0 to 63
- hist_ranks: int32 [512], P(('ctx', 'qry')), may hold values from 0 to 511, each once
- query_bins: int32 [32768, 16], P(('ctx', 'qry')), may hold values from 0 to 63
- bin_table: bfloat16 [1024, 512], replicated, may hold values from -4.5 to 4.5
- rank_vector: bfloat16 [512], replicated, may hold values from -5 to 5
- w_query: bfloat16 [512, 512], replicated, may hold values from -5.833631 to 5.833631
- w_key: bfloat16 [512, 512], replicated, may hold values from -0.176776695 to 0.176776695
- w_value: bfloat16 [512, 512], replicated, may hold values from -0.25 to 0.25
- w_out: bfloat16 [512, 512], replicated, may hold values from -0.25 to 0.25
- w_up: bfloat16 [512, 2048], replicated, may hold values from -0.25 to 0.25
- w_down: bfloat16 [2048, 512], replicated, may hold values from -0.125 to 0.125
Outputs:
- hist_out: bfloat16 [512, 512], P(('ctx', 'qry'))
- query_out: bfloat16 [32768, 512], P(('ctx', 'qry'))
The draws below stay inside these ranges and needn't reach their ends.
All inputs are finite; a program needn't handle non-finite values.
Results may differ from the reference program's by a relative error of at most 0.008.
Values may be sent and summed in bfloat16 or wider, within the bound.
A program may use at most 64 MiB of HBM per device.

```python
import math
import jax
import jax.numpy as jnp
from jax import lax

D = 512
HEADS = 8
FF = 2048
FEATURES = 16
BINS = 64
HISTORY = 512
QUERIES = 32768


def paired_weights(key):
    folded = jax.random.fold_in(key, 7)
    key_shared, key_jitter = jax.random.split(folded, 2)
    shared = jax.random.truncated_normal(key_shared, -4.0, 4.0, (D, D), jnp.float32) * (1.0 / math.sqrt(D))
    jitter = jax.random.truncated_normal(key_jitter, -4.0, 4.0, (D, D), jnp.float32) * (1.0 / math.sqrt(D))
    queried = 3.0 * jitter
    return (queried, shared)


def draw_w_query(key, part):
    return paired_weights(key)[0].astype(jnp.bfloat16)


def draw_w_key(key, part):
    return paired_weights(key)[1].astype(jnp.bfloat16)


def draw_bin_table(key, part):
    folded = jax.random.fold_in(key, 11)
    key_rows, key_cols, key_values = jax.random.split(folded, 3)
    row_scale = jnp.exp(jax.random.uniform(key_rows, (FEATURES * BINS, 1), jnp.float32, math.log(0.3), math.log(1.5)))
    col_scale = jnp.exp(jax.random.uniform(key_cols, (1, D), jnp.float32, math.log(0.3), math.log(3.0)))
    entries = jax.random.truncated_normal(key_values, -4.0, 4.0, (FEATURES * BINS, D), jnp.float32)
    return (0.25 * entries * row_scale * col_scale).astype(jnp.bfloat16)


def with_ends(values, stream_key, least, largest):
    longest = values.shape.index(max(values.shape))
    spots = []
    for shift in (0, 1):
        where = [jax.random.randint(jax.random.fold_in(stream_key, axis), (), 0, length) for axis, length in enumerate(values.shape)]
        where[longest] = (where[longest] + shift) % values.shape[longest]
        spots.append(tuple(where))
    return values.at[spots[0]].set(least).at[spots[1]].set(largest)


def bell_draw(stream_key, shape, spread, limit, kind=jnp.bfloat16):
    values = jax.random.normal(stream_key, shape, jnp.float32) * spread
    return jnp.minimum(jnp.maximum(values, -limit), limit).astype(kind)


def setup_inputs(seed: int = 0) -> dict:
    keys = jax.random.split(jax.random.key(seed), 12)
    return {
        "hist_bins": with_ends(jax.random.randint(keys[0], (HISTORY, FEATURES), 0, BINS), jax.random.fold_in(keys[0], 1), 0, BINS - 1).astype(jnp.int32),
        "hist_ranks": jax.random.permutation(keys[1], HISTORY).astype(jnp.int32),
        "query_bins": with_ends(jax.random.randint(keys[2], (QUERIES, FEATURES), 0, BINS), jax.random.fold_in(keys[2], 1), 0, BINS - 1).astype(jnp.int32),
        "bin_table": draw_bin_table(jax.random.fold_in(keys[11], 71), 0),
        "rank_vector": bell_draw(keys[4], (D,), 1.0, 5.0),
        "w_query": draw_w_query(jax.random.fold_in(keys[11], 71), 0),
        "w_key": draw_w_key(jax.random.fold_in(keys[11], 71), 0),
        "w_value": bell_draw(keys[7], (D, D), D ** -0.5, 0.25),
        "w_out": bell_draw(keys[8], (D, D), D ** -0.5, 0.25),
        "w_up": bell_draw(keys[9], (D, FF), D ** -0.5, 0.25),
        "w_down": bell_draw(keys[10], (FF, D), FF ** -0.5, 0.125),
    }


epsilon = 1e-05

def normalize(values):
    centered = values - lax.optimization_barrier(jnp.mean(values, axis=-1, keepdims=True))
    variance = lax.optimization_barrier(jnp.mean(centered * centered, axis=-1, keepdims=True))
    return centered * lax.rsqrt(variance + epsilon)

def embed_bins(bin_rows, bin_table):
    summed = jnp.zeros((bin_rows.shape[0], bin_table.shape[1]), jnp.float32)
    for feature in range(bin_rows.shape[1]):
        looked_up = jnp.take(bin_table, (bin_rows[:, feature] + feature * BINS).astype(jnp.int32), axis=0)
        summed = summed + looked_up.astype(jnp.float32)
    return summed

def history_rows(bin_rows, rank_ids, bin_table, rank_vector, history_total):
    level = (2.0 * rank_ids.astype(jnp.float32) + 1.0) / history_total - 1.0
    return embed_bins(bin_rows, bin_table) + level[:, None] * rank_vector.astype(jnp.float32)[None, :]

def attend_all(queries, key_rows, value_rows):
    row_count = queries.shape[0]
    head_dim = queries.shape[1] // HEADS
    query_heads = queries.reshape(row_count, HEADS, head_dim).astype(jnp.float32)
    key_heads = key_rows.reshape(-1, HEADS, head_dim).astype(jnp.float32)
    value_heads = value_rows.reshape(-1, HEADS, head_dim).astype(jnp.float32)
    scores = jnp.einsum('nhd,khd->hnk', query_heads, key_heads) * head_dim ** (-0.5)
    row_peak = lax.optimization_barrier(jnp.max(scores, axis=-1, keepdims=True))
    weights = jnp.exp(scores - row_peak)
    row_total = lax.optimization_barrier(jnp.sum(weights, axis=-1))
    rounded = lax.optimization_barrier(weights.astype(jnp.bfloat16)).astype(jnp.float32)
    summed = jnp.einsum('hnk,khd->hnd', rounded, value_heads) / row_total[..., None]
    return jnp.transpose(summed, (1, 0, 2)).reshape(row_count, -1).astype(jnp.bfloat16)

def layer_rows(all_rows, key_rows, value_rows, w_query, w_out, w_up, w_down):
    normed = normalize(all_rows).astype(jnp.bfloat16)
    queries = jnp.dot(normed, w_query, preferred_element_type=jnp.float32).astype(jnp.bfloat16)
    attended = attend_all(queries, key_rows, value_rows)
    after_attention = all_rows + jnp.dot(attended, w_out, preferred_element_type=jnp.float32)
    inner = jnp.dot(normalize(after_attention).astype(jnp.bfloat16), w_up, preferred_element_type=jnp.float32)
    hidden = jax.nn.gelu(inner, approximate=True).astype(jnp.bfloat16)
    return (after_attention + jnp.dot(hidden, w_down, preferred_element_type=jnp.float32)).astype(jnp.bfloat16)

def reference(hist_bins, hist_ranks, query_bins, bin_table, rank_vector, w_query, w_key, w_value, w_out, w_up, w_down):
    hist_embed = history_rows(hist_bins, hist_ranks, bin_table, rank_vector, float(HISTORY))
    hist_normed = normalize(hist_embed).astype(jnp.bfloat16)
    key_rows = jnp.dot(hist_normed, w_key, preferred_element_type=jnp.float32).astype(jnp.bfloat16)
    value_rows = jnp.dot(hist_normed, w_value, preferred_element_type=jnp.float32).astype(jnp.bfloat16)

    def apply_layer(block_rows):
        return layer_rows(block_rows, key_rows, value_rows, w_query, w_out, w_up, w_down)
    hist_size = math.gcd(hist_embed.shape[0], 512)
    hist_blocks = hist_embed.reshape(-1, hist_size, hist_embed.shape[1])
    hist_out = lax.map(apply_layer, hist_blocks).reshape(hist_embed.shape[0], -1)

    def query_block(bin_rows):
        return apply_layer(embed_bins(bin_rows, bin_table))
    query_size = math.gcd(query_bins.shape[0], 512)
    query_blocks = query_bins.reshape(-1, query_size, query_bins.shape[1])
    query_out = lax.map(query_block, query_blocks).reshape(query_bins.shape[0], -1)
    return (hist_out, query_out)
```

```python
import functools
import math

import jax
import jax.numpy as jnp
from jax import lax
from jax.experimental import pallas as pl
from jax.experimental.pallas import tpu as pltpu
from jax.sharding import PartitionSpec as P

HEADS = 8
LANES = 128
RADIX = 64
epsilon = 1e-05
F32 = jnp.float32
BF16 = jnp.bfloat16


def normalize(values):
    centered = values - jnp.mean(values, axis=-1, keepdims=True)
    variance = jnp.mean(centered * centered, axis=-1, keepdims=True)
    return centered * lax.rsqrt(variance + epsilon)


def dot(a, b):
    return jnp.dot(a, b, preferred_element_type=F32)


def embed(bins, spread, column_bin, table):
    named = dot(bins, spread)
    one_hot = jnp.where(named == column_bin, 1.0, 0.0).astype(BF16)
    return dot(one_hot, table)


def embed_kernel(
    sizes,
    query_bins,
    hist_bins,
    hist_ranks,
    table,
    rank_vector,
    w_query,
    w_key,
    w_value,
    rows_out,
    queries_out,
    keys_out,
    values_out,
    staged,
    mine,
    blocks,
    hist_rows,
    hist_normed,
    send_sem,
    recv_sem,
):
    inner, count, query_tile, hist_tile = sizes
    own, features = hist_bins.shape
    query_count = query_bins.shape[0]
    total = count * own
    me = lax.axis_index("ctx") * inner + lax.axis_index("qry")

    def place(index):
        return {"ctx": index // inner, "qry": index % inner}

    def partner(step):
        return (me + step) % count

    barrier = pltpu.get_barrier_semaphore()

    def greet(step, carry):
        pl.semaphore_signal(
            barrier,
            inc=1,
            device_id=place(partner(step)),
            device_id_type=pl.DeviceIdType.MESH,
        )
        return carry

    lax.fori_loop(1, count, greet, 0)

    ranks = jnp.broadcast_to(hist_ranks[...], (own, own))
    diagonal = lax.broadcasted_iota(jnp.int32, (own, own), 0) == lax.broadcasted_iota(
        jnp.int32, (own, own), 1
    )
    rank = jnp.sum(jnp.where(diagonal, ranks.astype(F32), 0.0), axis=1, keepdims=True)
    high = jnp.floor(rank * (1.0 / RADIX))
    staged[...] = jnp.zeros_like(staged)
    staged[:, :features] = hist_bins[...].astype(F32)
    staged[:, features : features + 1] = high
    staged[:, features + 1 : features + 2] = rank - high * RADIX
    mine[...] = staged[...].astype(BF16)
    blocks[me] = mine[...]

    bin_count = table.shape[0] // features
    wide = (features, table.shape[0])
    spread = jnp.where(
        lax.broadcasted_iota(jnp.int32, wide, 1) // bin_count
        == lax.broadcasted_iota(jnp.int32, wide, 0),
        1.0,
        0.0,
    ).astype(BF16)
    column_bin = (
        lax.broadcasted_iota(jnp.int32, (1, table.shape[0]), 1) % bin_count
    ).astype(F32)

    def copy_to(step):
        other = partner(step)
        return pltpu.make_async_remote_copy(
            src_ref=mine,
            dst_ref=blocks.at[me],
            send_sem=send_sem.at[other],
            recv_sem=recv_sem.at[me],
            device_id=place(other),
            device_id_type=pl.DeviceIdType.MESH,
        )

    def copy_from(step):
        other = partner(step)
        return pltpu.make_async_remote_copy(
            src_ref=mine,
            dst_ref=blocks.at[other],
            send_sem=send_sem.at[other],
            recv_sem=recv_sem.at[other],
            device_id=place(other),
            device_id_type=pl.DeviceIdType.MESH,
        )

    def send(step, carry):
        copy_to(step).start()
        return carry

    pl.semaphore_wait(barrier, count - 1)
    lax.fori_loop(1, count, send, 0)

    def query_step(index, carry):
        at = pl.ds(pl.multiple_of(index * query_tile, query_tile), query_tile)
        found = embed(query_bins[at, :].astype(F32).astype(BF16), spread, column_bin, table[...])
        rows_out[at, :] = found
        queries_out[at, :] = dot(normalize(found).astype(BF16), w_query[...]).astype(BF16)
        return carry

    lax.fori_loop(0, query_count // query_tile, query_step, 0)

    def finish(step, carry):
        copy_to(step).wait_send()
        copy_from(step).wait_recv()
        return carry

    lax.fori_loop(1, count, finish, 0)

    def hist_step(index, carry):
        tile_blocks = hist_tile // own
        block = blocks[pl.ds(index * tile_blocks, tile_blocks)].reshape(hist_tile, LANES)
        at = pl.ds(pl.multiple_of(index * hist_tile, hist_tile), hist_tile)
        wide_block = block.astype(F32)
        rank = (
            wide_block[:, features : features + 1] * RADIX
            + wide_block[:, features + 1 : features + 2]
        )
        level = (2.0 * rank + 1.0) / float(total) - 1.0
        found = embed(block[:, :features], spread, column_bin, table[...])
        found = found + level * rank_vector[...].astype(F32)
        hist_rows[at, :] = found
        normed = normalize(found).astype(BF16)
        hist_normed[at, :] = normed
        keys_out[index] = dot(normed, w_key[...]).T.astype(BF16)
        values_out[index] = dot(normed, w_value[...]).astype(BF16)
        return carry

    lax.fori_loop(0, total // hist_tile, hist_step, 0)
    at = pl.ds(pl.multiple_of(me * own, own), own)
    rows_out[query_count:, :] = hist_rows[at, :]
    queries_out[query_count:, :] = dot(hist_normed[at, :], w_query[...]).astype(BF16)


def layer_kernel(
    sizes,
    rows,
    queries,
    keys,
    values,
    w_out,
    w_up,
    w_down,
    query_out,
    hist_out,
    key_pairs,
    value_pairs,
):
    own, ff_tile = sizes
    chunks, width, key_count = keys.shape
    head_dim = width // HEADS
    pairs = HEADS // 2
    tile = rows.shape[0]
    factor = math.log2(math.e) * head_dim ** (-0.5)

    @pl.when(pl.program_id(0) == 0)
    def _():
        left = lax.broadcasted_iota(jnp.int32, (key_count, LANES), 1) < head_dim
        upper = lax.broadcasted_iota(jnp.int32, (LANES, key_count), 0) < head_dim
        one = jnp.ones((key_count, LANES), F32)

        def arrange(chunk, carry):
            for pair in range(pairs):
                span = slice(pair * LANES, (pair + 1) * LANES)
                key = keys[chunk, span, :].astype(F32)
                key_pairs[chunk, pair, :, :key_count] = jnp.where(upper, key, 0.0).astype(BF16)
                key_pairs[chunk, pair, :, key_count:] = jnp.where(upper, 0.0, key).astype(BF16)
                value = values[chunk, :, span].astype(F32)
                for half, top in ((0, True), (1, False)):
                    at = slice(half * key_count, (half + 1) * key_count)
                    keep = left if top else jnp.logical_not(left)
                    value_pairs[chunk, pair, at, :LANES] = jnp.where(keep, value, 0.0).astype(BF16)
                    value_pairs[chunk, pair, at, LANES:] = jnp.where(keep, one, 0.0).astype(BF16)
            return carry

        lax.fori_loop(0, chunks, arrange, 0)

    def pair_scores(chunk, pair):
        scores = dot(queries[:, pair * LANES : (pair + 1) * LANES], key_pairs[chunk, pair])
        return scores[:, :key_count], scores[:, key_count:]

    def weigh(scores, peak):
        return jnp.exp2((scores - peak) * factor).astype(BF16)

    attended = []
    for pair in range(pairs):
        even, odd = pair_scores(0, pair)
        peaks = [jnp.max(even, axis=1, keepdims=True), jnp.max(odd, axis=1, keepdims=True)]
        weights = jnp.concatenate([weigh(even, peaks[0]), weigh(odd, peaks[1])], axis=1)
        summed = dot(weights, value_pairs[0, pair])
        if chunks > 1:

            def absorb(chunk, carry, pair=pair):
                peak_even, peak_odd, summed = carry
                even, odd = pair_scores(chunk, pair)
                new_even = jnp.maximum(peak_even, jnp.max(even, axis=1, keepdims=True))
                new_odd = jnp.maximum(peak_odd, jnp.max(odd, axis=1, keepdims=True))
                weights = jnp.concatenate([weigh(even, new_even), weigh(odd, new_odd)], axis=1)
                lane = lax.broadcasted_iota(jnp.int32, summed.shape, 1) % LANES
                fade = jnp.where(
                    lane < head_dim,
                    jnp.exp2((peak_even - new_even) * factor),
                    jnp.exp2((peak_odd - new_odd) * factor),
                )
                summed = summed * fade + dot(weights, value_pairs[chunk, pair])
                return (new_even, new_odd, summed)

            summed = lax.fori_loop(1, chunks, absorb, (peaks[0], peaks[1], summed))[2]
        attended.append((summed[:, :LANES] / summed[:, LANES:]).astype(BF16))
    after = rows[...] + dot(jnp.concatenate(attended, axis=1), w_out[...])
    normed = normalize(after).astype(BF16)
    result = after
    for start in range(0, w_up.shape[1], ff_tile):
        inner = dot(normed, w_up[:, start : start + ff_tile])
        hidden = jax.nn.gelu(inner, approximate=True).astype(BF16)
        result = result + dot(hidden, w_down[start : start + ff_tile, :])
    result = result.astype(BF16)
    query_out[...] = result

    @pl.when(pl.program_id(0) == pl.num_programs(0) - 1)
    def _():
        hist_out[...] = result[tile - own :, :]


def local(
    inner,
    count,
    hist_bins,
    hist_ranks,
    query_bins,
    bin_table,
    rank_vector,
    w_query,
    w_key,
    w_value,
    w_out,
    w_up,
    w_down,
):
    own = hist_bins.shape[0]
    query_count = query_bins.shape[0]
    width = bin_table.shape[1]
    total = own * count
    row_count = own + query_count
    hist_tile = math.gcd(total, 512)
    query_tile = math.gcd(query_count, 256)
    chunks = total // hist_tile
    vmem = pl.BlockSpec(memory_space=pltpu.VMEM)
    rows, queries, keys, values = pl.pallas_call(
        functools.partial(embed_kernel, (inner, count, query_tile, hist_tile)),
        out_shape=(
            jax.ShapeDtypeStruct((row_count, width), F32),
            jax.ShapeDtypeStruct((row_count, width), BF16),
            jax.ShapeDtypeStruct((chunks, width, hist_tile), BF16),
            jax.ShapeDtypeStruct((chunks, hist_tile, width), BF16),
        ),
        in_specs=[vmem] * 8,
        out_specs=(vmem,) * 4,
        scratch_shapes=[
            pltpu.VMEM((own, LANES), F32),
            pltpu.VMEM((own, LANES), BF16),
            pltpu.VMEM((count, own, LANES), BF16),
            pltpu.VMEM((total, width), F32),
            pltpu.VMEM((total, width), BF16),
            pltpu.SemaphoreType.DMA((count,)),
            pltpu.SemaphoreType.DMA((count,)),
        ],
        compiler_params=pltpu.CompilerParams(
            collective_id=0, has_side_effects=True, vmem_limit_bytes=40 << 20
        ),
        name="embed_rows",
    )(
        query_bins,
        hist_bins,
        hist_ranks.reshape(1, own),
        bin_table,
        rank_vector.reshape(1, width),
        w_query,
        w_key,
        w_value,
    )
    tile = max(
        size for size in range(16, 257, 16) if row_count % size == 0 and size >= own
    )

    def whole(shape):
        return pl.BlockSpec(
            shape, lambda i: (0,) * len(shape), pipeline_mode=pl.Buffered(1)
        )

    query_out, hist_out = pl.pallas_call(
        functools.partial(layer_kernel, (own, min(512, w_up.shape[1]))),
        out_shape=(
            jax.ShapeDtypeStruct((query_count, width), BF16),
            jax.ShapeDtypeStruct((own, width), BF16),
        ),
        grid=(row_count // tile,),
        in_specs=[
            pl.BlockSpec((tile, width), lambda i: (i, 0)),
            pl.BlockSpec((tile, width), lambda i: (i, 0)),
            whole(keys.shape),
            whole(values.shape),
            whole(w_out.shape),
            whole(w_up.shape),
            whole(w_down.shape),
        ],
        out_specs=(
            pl.BlockSpec((tile, width), lambda i: (i, 0)),
            pl.BlockSpec((own, width), lambda i: (0, 0)),
        ),
        scratch_shapes=[
            pltpu.VMEM((chunks, HEADS // 2, LANES, 2 * hist_tile), BF16),
            pltpu.VMEM((chunks, HEADS // 2, 2 * hist_tile, 2 * LANES), BF16),
        ],
        compiler_params=pltpu.CompilerParams(vmem_limit_bytes=56 << 20),
        name="layer_rows",
    )(rows, queries, keys, values, w_out, w_up, w_down)
    return (hist_out, query_out)


def solution(mesh):
    inner = mesh.shape["qry"]
    split = P(("ctx", "qry"), None)
    return jax.shard_map(
        functools.partial(local, inner, mesh.shape["ctx"] * inner),
        mesh=mesh,
        in_specs=(split, P(("ctx", "qry")), split) + (P(),) * 8,
        out_specs=(split, split),
        check_vma=False,
    )
```

```python
import functools
import math

import jax
import jax.numpy as jnp
from jax import lax
from jax.experimental import pallas as pl
from jax.experimental.pallas import tpu as pltpu
from jax.sharding import PartitionSpec as P

HEADS = 8
LANES = 128
RADIX = 64
VMEM_LIMIT = 64 << 20
epsilon = 1e-05
F32 = jnp.float32
BF16 = jnp.bfloat16


def normalize(values):
    centered = values - jnp.mean(values, axis=-1, keepdims=True)
    variance = jnp.mean(centered * centered, axis=-1, keepdims=True)
    return centered * lax.rsqrt(variance + epsilon)


def dot(a, b):
    return jnp.dot(a, b, preferred_element_type=F32)


def embed(named, column_bin, table):
    one_hot = jnp.where(named == column_bin, 1.0, 0.0).astype(BF16)
    return dot(one_hot, table)


def layer_kernel(
    sizes,
    query_bins_hbm,
    hist_bins_hbm,
    hist_ranks_hbm,
    table_hbm,
    rank_vector_hbm,
    w_query_hbm,
    w_key_hbm,
    w_value_hbm,
    w_out_hbm,
    w_up_hbm,
    w_down_hbm,
    hist_out,
    query_out,
    query_bins,
    hist_bins,
    hist_ranks,
    table,
    rank_vector,
    w_query,
    w_key,
    w_value,
    w_out,
    w_up,
    w_down,
    fetch_sem,
    store_sem,
    rows_out,
    queries_out,
    results,
    key_pairs,
    value_pairs,
    staged,
    mine,
    blocks,
    hist_rows,
    hist_normed,
    send_sem,
    recv_sem,
):
    inner, count, query_tile, hist_tile, tile, ff_tile = sizes
    own, features = hist_bins.shape
    query_count = query_bins.shape[1]
    total = count * own
    fetches = [
        pltpu.make_async_copy(source, target, fetch_sem.at[index])
        for index, (source, target) in enumerate(
            (
                (hist_bins_hbm, hist_bins),
                (hist_ranks_hbm, hist_ranks),
                (query_bins_hbm, query_bins),
                (table_hbm, table),
                (w_query_hbm, w_query),
                (rank_vector_hbm, rank_vector),
                (w_key_hbm, w_key),
                (w_value_hbm, w_value),
                (w_out_hbm, w_out),
                (w_up_hbm, w_up),
                (w_down_hbm, w_down),
            )
        )
    ]
    for fetch in fetches:
        fetch.start()
    me = lax.axis_index("ctx") * inner + lax.axis_index("qry")

    def place(index):
        return {"ctx": index // inner, "qry": index % inner}

    def partner(step):
        return (me + step) % count

    barrier = pltpu.get_barrier_semaphore()

    def greet(step, carry):
        pl.semaphore_signal(
            barrier,
            inc=1,
            device_id=place(partner(step)),
            device_id_type=pl.DeviceIdType.MESH,
        )
        return carry

    lax.fori_loop(1, count, greet, 0)

    fetches[0].wait()
    fetches[1].wait()
    ranks = jnp.broadcast_to(hist_ranks[...], (own, own))
    diagonal = lax.broadcasted_iota(jnp.int32, (own, own), 0) == lax.broadcasted_iota(
        jnp.int32, (own, own), 1
    )
    rank = jnp.sum(jnp.where(diagonal, ranks.astype(F32), 0.0), axis=1, keepdims=True)
    high = jnp.floor(rank * (1.0 / RADIX))
    staged[...] = jnp.zeros_like(staged)
    staged[:, :features] = hist_bins[...].astype(F32)
    staged[:, features : features + 1] = high
    staged[:, features + 1 : features + 2] = rank - high * RADIX
    mine[...] = staged[...].astype(BF16)
    blocks[me] = mine[...]

    bin_count = table.shape[0] // features
    wide = (features, table.shape[0])
    spread = jnp.where(
        lax.broadcasted_iota(jnp.int32, wide, 1) // bin_count
        == lax.broadcasted_iota(jnp.int32, wide, 0),
        1.0,
        0.0,
    ).astype(BF16)
    column_bin = (
        lax.broadcasted_iota(jnp.int32, (1, table.shape[0]), 1) % bin_count
    ).astype(F32)

    def copy_to(step):
        other = partner(step)
        return pltpu.make_async_remote_copy(
            src_ref=mine,
            dst_ref=blocks.at[me],
            send_sem=send_sem.at[other],
            recv_sem=recv_sem.at[me],
            device_id=place(other),
            device_id_type=pl.DeviceIdType.MESH,
        )

    def copy_from(step):
        other = partner(step)
        return pltpu.make_async_remote_copy(
            src_ref=mine,
            dst_ref=blocks.at[other],
            send_sem=send_sem.at[other],
            recv_sem=recv_sem.at[other],
            device_id=place(other),
            device_id_type=pl.DeviceIdType.MESH,
        )

    def send(step, carry):
        copy_to(step).start()
        return carry

    pl.semaphore_wait(barrier, count - 1)
    lax.fori_loop(1, count, send, 0)

    for fetch in fetches[2:5]:
        fetch.wait()

    def query_step(index, carry):
        at = pl.ds(pl.multiple_of(index * query_tile, query_tile), query_tile)
        named = lax.dot_general(
            query_bins[:, at].astype(F32).astype(BF16),
            spread,
            (((0,), (0,)), ((), ())),
            preferred_element_type=F32,
        )
        found = embed(named, column_bin, table[...])
        rows_out[at, :] = found
        queries_out[at, :] = dot(normalize(found).astype(BF16), w_query[...]).astype(BF16)
        return carry

    lax.fori_loop(0, query_count // query_tile, query_step, 0)

    def finish(step, carry):
        copy_to(step).wait_send()
        copy_from(step).wait_recv()
        return carry

    for fetch in fetches[5:8]:
        fetch.wait()
    lax.fori_loop(1, count, finish, 0)

    width = table.shape[1]
    head_dim = width // HEADS
    pairs = HEADS // 2
    left = lax.broadcasted_iota(jnp.int32, (hist_tile, LANES), 1) < head_dim
    upper = lax.broadcasted_iota(jnp.int32, (LANES, hist_tile), 0) < head_dim

    def hist_step(index, carry):
        tile_blocks = hist_tile // own
        block = blocks[pl.ds(index * tile_blocks, tile_blocks)].reshape(hist_tile, LANES)
        at = pl.ds(pl.multiple_of(index * hist_tile, hist_tile), hist_tile)
        wide_block = block.astype(F32)
        rank = (
            wide_block[:, features : features + 1] * RADIX
            + wide_block[:, features + 1 : features + 2]
        )
        level = (2.0 * rank + 1.0) / float(total) - 1.0
        found = embed(dot(block[:, :features], spread), column_bin, table[...])
        found = found + level * rank_vector[...].astype(F32).reshape(1, -1)
        hist_rows[at, :] = found
        normed = normalize(found).astype(BF16)
        hist_normed[at, :] = normed
        keys = dot(normed, w_key[...]).T
        values = dot(normed, w_value[...])
        for pair in range(pairs):
            span = slice(pair * LANES, (pair + 1) * LANES)
            key = keys[span, :]
            key_pairs[index, pair, :, :hist_tile] = jnp.where(upper, key, 0.0).astype(BF16)
            key_pairs[index, pair, :, hist_tile:] = jnp.where(upper, 0.0, key).astype(BF16)
            value = values[:, span]
            for half, keep in ((0, left), (1, jnp.logical_not(left))):
                part = slice(half * hist_tile, (half + 1) * hist_tile)
                value_pairs[index, pair, part, :LANES] = jnp.where(keep, value, 0.0).astype(BF16)
                value_pairs[index, pair, part, LANES:] = jnp.where(keep, 1.0, 0.0).astype(BF16)
        return carry

    lax.fori_loop(0, total // hist_tile, hist_step, 0)
    at = pl.ds(pl.multiple_of(me * own, own), own)
    rows_out[query_count:, :] = hist_rows[at, :]
    queries_out[query_count:, :] = dot(hist_normed[at, :], w_query[...]).astype(BF16)

    factor = math.log2(math.e) * head_dim ** (-0.5)
    chunks = total // hist_tile
    tiles = (query_count + own) // tile
    for fetch in fetches[8:]:
        fetch.wait()

    def store(index):
        at = pl.ds(pl.multiple_of(index * tile, tile), tile)
        return pltpu.make_async_copy(results.at[at], query_out.at[at], store_sem.at[index])

    def pair_scores(at, chunk, pair):
        scores = dot(queries_out[at, pair * LANES : (pair + 1) * LANES], key_pairs[chunk, pair])
        return scores[:, :hist_tile], scores[:, hist_tile:]

    def weigh(scores, peak):
        return jnp.exp2((scores - peak) * factor).astype(BF16)

    def tile_step(index, carry):
        at = pl.ds(pl.multiple_of(index * tile, tile), tile)
        attended = []
        for pair in range(pairs):
            even, odd = pair_scores(at, 0, pair)
            peaks = [jnp.max(even, axis=1, keepdims=True), jnp.max(odd, axis=1, keepdims=True)]
            weights = jnp.concatenate([weigh(even, peaks[0]), weigh(odd, peaks[1])], axis=1)
            summed = dot(weights, value_pairs[0, pair])
            if chunks > 1:

                def absorb(chunk, carry, pair=pair):
                    peak_even, peak_odd, summed = carry
                    even, odd = pair_scores(at, chunk, pair)
                    new_even = jnp.maximum(peak_even, jnp.max(even, axis=1, keepdims=True))
                    new_odd = jnp.maximum(peak_odd, jnp.max(odd, axis=1, keepdims=True))
                    weights = jnp.concatenate([weigh(even, new_even), weigh(odd, new_odd)], axis=1)
                    lane = lax.broadcasted_iota(jnp.int32, summed.shape, 1) % LANES
                    fade = jnp.where(
                        lane < head_dim,
                        jnp.exp2((peak_even - new_even) * factor),
                        jnp.exp2((peak_odd - new_odd) * factor),
                    )
                    summed = summed * fade + dot(weights, value_pairs[chunk, pair])
                    return (new_even, new_odd, summed)

                summed = lax.fori_loop(1, chunks, absorb, (peaks[0], peaks[1], summed))[2]
            attended.append((summed[:, :LANES] / summed[:, LANES:]).astype(BF16))

        after = rows_out[at, :] + dot(jnp.concatenate(attended, axis=1), w_out[...])
        normed = normalize(after).astype(BF16)
        result = after
        for start in range(0, w_up.shape[1], ff_tile):
            inner = dot(normed, w_up[:, start : start + ff_tile])
            hidden = jax.nn.gelu(inner, approximate=True).astype(BF16)
            result = result + dot(hidden, w_down[start : start + ff_tile, :])
        results[at, :] = result.astype(BF16)

        @pl.when(index < tiles - 1)
        def _():
            store(index).start()

        return carry

    lax.fori_loop(0, tiles, tile_step, 0)
    last = slice((tiles - 1) * tile, query_count)
    ending = [
        pltpu.make_async_copy(results.at[last], query_out.at[last], store_sem.at[tiles - 1]),
        pltpu.make_async_copy(results.at[query_count:], hist_out, store_sem.at[tiles]),
    ]
    for part in ending:
        part.start()
    for index in range(tiles - 1):
        store(index).wait()
    for part in ending:
        part.wait()


def local(
    inner,
    count,
    hist_bins,
    hist_ranks,
    query_bins,
    bin_table,
    rank_vector,
    w_query,
    w_key,
    w_value,
    w_out,
    w_up,
    w_down,
):
    own = hist_bins.shape[0]
    query_count = query_bins.shape[0]
    width = bin_table.shape[1]
    total = own * count
    row_count = own + query_count
    hist_tile = math.gcd(total, 512)
    query_tile = math.gcd(query_count, 256)
    chunks = total // hist_tile
    features = hist_bins.shape[1]
    pairs = HEADS // 2
    tile = max(
        size for size in range(16, 257, 16) if row_count % size == 0 and size > own
    )
    tiles = row_count // tile
    hbm = pl.BlockSpec(memory_space=pltpu.HBM)
    return pl.pallas_call(
        functools.partial(
            layer_kernel,
            (inner, count, query_tile, hist_tile, tile, min(512, w_up.shape[1])),
        ),
        out_shape=(
            jax.ShapeDtypeStruct((own, width), BF16),
            jax.ShapeDtypeStruct((query_count, width), BF16),
        ),
        in_specs=[hbm] * 11,
        out_specs=(hbm, hbm),
        scratch_shapes=[
            pltpu.VMEM((features, query_count), jnp.int32),
            pltpu.VMEM((own, features), jnp.int32),
            pltpu.VMEM((1, own), jnp.int32),
            pltpu.VMEM(bin_table.shape, BF16),
            pltpu.VMEM(rank_vector.shape, BF16),
            pltpu.VMEM(w_query.shape, BF16),
            pltpu.VMEM(w_key.shape, BF16),
            pltpu.VMEM(w_value.shape, BF16),
            pltpu.VMEM(w_out.shape, BF16),
            pltpu.VMEM(w_up.shape, BF16),
            pltpu.VMEM(w_down.shape, BF16),
            pltpu.SemaphoreType.DMA((11,)),
            pltpu.SemaphoreType.DMA((tiles + 1,)),
            pltpu.VMEM((row_count, width), F32),
            pltpu.VMEM((row_count, width), BF16),
            pltpu.VMEM((row_count, width), BF16),
            pltpu.VMEM((chunks, pairs, LANES, 2 * hist_tile), BF16),
            pltpu.VMEM((chunks, pairs, 2 * hist_tile, 2 * LANES), BF16),
            pltpu.VMEM((own, LANES), F32),
            pltpu.VMEM((own, LANES), BF16),
            pltpu.VMEM((count, own, LANES), BF16),
            pltpu.VMEM((total, width), F32),
            pltpu.VMEM((total, width), BF16),
            pltpu.SemaphoreType.DMA((count,)),
            pltpu.SemaphoreType.DMA((count,)),
        ],
        compiler_params=pltpu.CompilerParams(
            collective_id=0, has_side_effects=True, vmem_limit_bytes=VMEM_LIMIT
        ),
        name="layer_rows",
    )(
        query_bins.T,
        hist_bins,
        hist_ranks.reshape(1, own),
        bin_table,
        rank_vector,
        w_query,
        w_key,
        w_value,
        w_out,
        w_up,
        w_down,
    )


def solution(mesh):
    inner = mesh.shape["qry"]
    split = P(("ctx", "qry"), None)
    return jax.shard_map(
        functools.partial(local, inner, mesh.shape["ctx"] * inner),
        mesh=mesh,
        in_specs=(split, P(("ctx", "qry")), split) + (P(),) * 8,
        out_specs=(split, split),
        check_vma=False,
    )
```

```python
import functools
import math

import jax
import jax.numpy as jnp
from jax import lax
from jax.experimental import pallas as pl
from jax.experimental.pallas import tpu as pltpu
from jax.sharding import PartitionSpec as P

HEADS = 8
LANES = 128
RADIX = 64
VMEM_LIMIT = 64 << 20
epsilon = 1e-05
F32 = jnp.float32
BF16 = jnp.bfloat16


def normalize(values):
    centered = values - jnp.mean(values, axis=-1, keepdims=True)
    variance = jnp.mean(centered * centered, axis=-1, keepdims=True)
    return centered * lax.rsqrt(variance + epsilon)


def dot(a, b):
    return jnp.dot(a, b, preferred_element_type=F32)


def embed(named, column_bin, table):
    one_hot = jnp.where(named == column_bin, 1.0, 0.0).astype(BF16)
    return dot(one_hot, table)


def layer_kernel(
    sizes,
    query_bins_hbm,
    hist_bins_hbm,
    hist_ranks_hbm,
    table_hbm,
    rank_vector_hbm,
    w_query_hbm,
    w_key_hbm,
    w_value_hbm,
    w_out_hbm,
    w_up_hbm,
    w_down_hbm,
    hist_out,
    query_out,
    query_bins,
    hist_bins,
    hist_ranks,
    table,
    rank_vector,
    w_query,
    w_key,
    w_value,
    w_out,
    w_up,
    w_down,
    fetch_sem,
    store_sem,
    results,
    rows_out,
    queries_out,
    key_pairs,
    value_pairs,
    staged,
    mine,
    blocks,
    hist_rows,
    hist_normed,
    send_sem,
    recv_sem,
):
    inner, count, query_tile, hist_tile, tile = sizes
    own, features = hist_bins.shape
    query_count = query_bins.shape[1]
    total = count * own
    fetches = [
        pltpu.make_async_copy(source, target, fetch_sem.at[index])
        for index, (source, target) in enumerate(
            (
                (hist_bins_hbm, hist_bins),
                (hist_ranks_hbm, hist_ranks),
                (query_bins_hbm, query_bins),
                (table_hbm, table),
                (w_query_hbm, w_query),
                (rank_vector_hbm, rank_vector),
                (w_key_hbm, w_key),
                (w_value_hbm, w_value),
                (w_out_hbm, w_out),
                (w_up_hbm, w_up),
                (w_down_hbm, w_down),
            )
        )
    ]
    for fetch in fetches:
        fetch.start()
    me = lax.axis_index("ctx") * inner + lax.axis_index("qry")

    def place(index):
        return {"ctx": index // inner, "qry": index % inner}

    def partner(step):
        return (me + step) % count

    barrier = pltpu.get_barrier_semaphore()

    def greet(step, carry):
        pl.semaphore_signal(
            barrier,
            inc=1,
            device_id=place(partner(step)),
            device_id_type=pl.DeviceIdType.MESH,
        )
        return carry

    lax.fori_loop(1, count, greet, 0)

    fetches[0].wait()
    fetches[1].wait()
    ranks = jnp.broadcast_to(hist_ranks[...], (own, own))
    diagonal = lax.broadcasted_iota(jnp.int32, (own, own), 0) == lax.broadcasted_iota(
        jnp.int32, (own, own), 1
    )
    rank = jnp.sum(jnp.where(diagonal, ranks.astype(F32), 0.0), axis=1, keepdims=True)
    high = jnp.floor(rank * (1.0 / RADIX))
    staged[...] = jnp.zeros_like(staged)
    staged[:, :features] = hist_bins[...].astype(F32)
    staged[:, features : features + 1] = high
    staged[:, features + 1 : features + 2] = rank - high * RADIX
    mine[...] = staged[...].astype(BF16)
    blocks[me] = mine[...]

    bin_count = table.shape[0] // features
    wide = (features, table.shape[0])
    spread = jnp.where(
        lax.broadcasted_iota(jnp.int32, wide, 1) // bin_count
        == lax.broadcasted_iota(jnp.int32, wide, 0),
        1.0,
        0.0,
    ).astype(BF16)
    column_bin = (
        lax.broadcasted_iota(jnp.int32, (1, table.shape[0]), 1) % bin_count
    ).astype(F32)

    def copy_to(step):
        other = partner(step)
        return pltpu.make_async_remote_copy(
            src_ref=mine,
            dst_ref=blocks.at[me],
            send_sem=send_sem.at[other],
            recv_sem=recv_sem.at[me],
            device_id=place(other),
            device_id_type=pl.DeviceIdType.MESH,
        )

    def copy_from(step):
        other = partner(step)
        return pltpu.make_async_remote_copy(
            src_ref=mine,
            dst_ref=blocks.at[other],
            send_sem=send_sem.at[other],
            recv_sem=recv_sem.at[other],
            device_id=place(other),
            device_id_type=pl.DeviceIdType.MESH,
        )

    def send(step, carry):
        copy_to(step).start()
        return carry

    pl.semaphore_wait(barrier, count - 1)
    lax.fori_loop(1, count, send, 0)

    for fetch in fetches[2:5]:
        fetch.wait()

    def query_step(index, carry):
        at = pl.ds(pl.multiple_of(index * query_tile, query_tile), query_tile)
        named = lax.dot_general(
            query_bins[:, at].astype(F32).astype(BF16),
            spread,
            (((0,), (0,)), ((), ())),
            preferred_element_type=F32,
        )
        found = embed(named, column_bin, table[...])
        rows_out[at, :] = found
        queries_out[at, :] = dot(normalize(found).astype(BF16), w_query[...]).astype(BF16)
        return carry

    lax.fori_loop(0, query_count // query_tile, query_step, 0, unroll=True)

    def finish(step, carry):
        copy_to(step).wait_send()
        copy_from(step).wait_recv()
        return carry

    for fetch in fetches[5:8]:
        fetch.wait()
    lax.fori_loop(1, count, finish, 0)

    width = table.shape[1]
    head_dim = width // HEADS
    pairs = HEADS // 2
    left = lax.broadcasted_iota(jnp.int32, (hist_tile, LANES), 1) < head_dim
    upper = lax.broadcasted_iota(jnp.int32, (LANES, hist_tile), 0) < head_dim

    def hist_step(index, carry):
        tile_blocks = hist_tile // own
        block = blocks[pl.ds(index * tile_blocks, tile_blocks)].reshape(hist_tile, LANES)
        at = pl.ds(pl.multiple_of(index * hist_tile, hist_tile), hist_tile)
        wide_block = block.astype(F32)
        rank = (
            wide_block[:, features : features + 1] * RADIX
            + wide_block[:, features + 1 : features + 2]
        )
        level = (2.0 * rank + 1.0) / float(total) - 1.0
        found = embed(dot(block[:, :features], spread), column_bin, table[...])
        found = found + level * rank_vector[...].astype(F32).reshape(1, -1)
        hist_rows[at, :] = found
        normed = normalize(found).astype(BF16)
        hist_normed[at, :] = normed
        keys = dot(normed, w_key[...]).T
        values = dot(normed, w_value[...])
        for pair in range(pairs):
            span = slice(pair * LANES, (pair + 1) * LANES)
            key = keys[span, :]
            key_pairs[index, pair, :, :hist_tile] = jnp.where(upper, key, 0.0).astype(BF16)
            key_pairs[index, pair, :, hist_tile:] = jnp.where(upper, 0.0, key).astype(BF16)
            value = values[:, span]
            for half, keep in ((0, left), (1, jnp.logical_not(left))):
                part = slice(half * hist_tile, (half + 1) * hist_tile)
                value_pairs[index, pair, part, :LANES] = jnp.where(keep, value, 0.0).astype(BF16)
                value_pairs[index, pair, part, LANES:] = jnp.where(keep, 1.0, 0.0).astype(BF16)
        return carry

    lax.fori_loop(0, total // hist_tile, hist_step, 0)
    at = pl.ds(pl.multiple_of(me * own, own), own)
    rows_out[query_count:, :] = hist_rows[at, :]
    queries_out[query_count:, :] = dot(hist_normed[at, :], w_query[...]).astype(BF16)

    factor = math.log2(math.e) * head_dim ** (-0.5)
    chunks = total // hist_tile
    tiles = (query_count + own) // tile
    for fetch in fetches[8:]:
        fetch.wait()

    def pair_scores(at, chunk, pair):
        scores = dot(queries_out[at, pair * LANES : (pair + 1) * LANES], key_pairs[chunk, pair])
        return scores[:, :hist_tile], scores[:, hist_tile:]

    def weigh(scores, peak):
        return jnp.exp2((scores - peak) * factor).astype(BF16)

    def attend(at, pair):
        even, odd = pair_scores(at, 0, pair)
        peaks = [jnp.max(even, axis=1, keepdims=True), jnp.max(odd, axis=1, keepdims=True)]
        weights = jnp.concatenate([weigh(even, peaks[0]), weigh(odd, peaks[1])], axis=1)
        summed = dot(weights, value_pairs[0, pair])
        if chunks > 1:

            def absorb(chunk, carry):
                peak_even, peak_odd, summed = carry
                even, odd = pair_scores(at, chunk, pair)
                new_even = jnp.maximum(peak_even, jnp.max(even, axis=1, keepdims=True))
                new_odd = jnp.maximum(peak_odd, jnp.max(odd, axis=1, keepdims=True))
                weights = jnp.concatenate([weigh(even, new_even), weigh(odd, new_odd)], axis=1)
                lane = lax.broadcasted_iota(jnp.int32, summed.shape, 1) % LANES
                fade = jnp.where(
                    lane < head_dim,
                    jnp.exp2((peak_even - new_even) * factor),
                    jnp.exp2((peak_odd - new_odd) * factor),
                )
                summed = summed * fade + dot(weights, value_pairs[chunk, pair])
                return (new_even, new_odd, summed)

            summed = lax.fori_loop(1, chunks, absorb, (peaks[0], peaks[1], summed))[2]
        return (summed[:, :LANES] / summed[:, LANES:]).astype(BF16)

    def project(at, attended):
        after = rows_out[at, :] + dot(jnp.concatenate(attended, axis=1), w_out[...])
        rows_out[at, :] = after
        queries_out[at, :] = normalize(after).astype(BF16)

    ff_tile = w_up.shape[1] // pairs

    def feed(normed, part):
        span = slice(part * ff_tile, (part + 1) * ff_tile)
        hidden = jax.nn.gelu(dot(normed, w_up[:, span]), approximate=True).astype(BF16)
        return dot(hidden, w_down[span, :])

    def rows_at(index):
        return pl.ds(pl.multiple_of(index * tile, tile), tile)

    def store(index):
        at = rows_at(index)
        return pltpu.make_async_copy(results.at[at], query_out.at[at], store_sem.at[index])

    first = slice(0, tile)
    project(first, [attend(first, pair) for pair in range(pairs)])

    def tile_step(index, carry):
        at, before = rows_at(index), rows_at(index - 1)
        normed = queries_out[before, :]
        result = rows_out[before, :]
        attended = []
        for pair in range(pairs):
            attended.append(attend(at, pair))
            if pair < pairs - 1:
                result = result + feed(normed, pair)
        project(at, attended)
        results[before, :] = (result + feed(normed, pairs - 1)).astype(BF16)
        store(index - 1).start()
        return carry

    lax.fori_loop(1, tiles, tile_step, 0)
    start = (tiles - 1) * tile
    normed = queries_out[start:, :]
    result = rows_out[start:, :]
    for part in range(pairs):
        result = result + feed(normed, part)
    result = result.astype(BF16)
    results[start:, :] = result
    last = slice(start, query_count)
    ending = [
        pltpu.make_async_copy(results.at[last], query_out.at[last], store_sem.at[tiles - 1]),
        pltpu.make_async_copy(results.at[query_count:], hist_out, store_sem.at[tiles]),
    ]
    for part in ending:
        part.start()
    for index in range(tiles - 1):
        store(index).wait()
    for part in ending:
        part.wait()


def local(
    inner,
    count,
    hist_bins,
    hist_ranks,
    query_bins,
    bin_table,
    rank_vector,
    w_query,
    w_key,
    w_value,
    w_out,
    w_up,
    w_down,
):
    own = hist_bins.shape[0]
    query_count = query_bins.shape[0]
    width = bin_table.shape[1]
    total = own * count
    row_count = own + query_count
    hist_tile = math.gcd(total, 512)
    query_tile = math.gcd(query_count, 256)
    chunks = total // hist_tile
    features = hist_bins.shape[1]
    pairs = HEADS // 2
    tile = max(
        size for size in range(16, 257, 16) if row_count % size == 0 and size > own
    )
    hbm = pl.BlockSpec(memory_space=pltpu.HBM)
    return pl.pallas_call(
        functools.partial(
            layer_kernel,
            (inner, count, query_tile, hist_tile, tile),
        ),
        out_shape=(
            jax.ShapeDtypeStruct((own, width), BF16),
            jax.ShapeDtypeStruct((query_count, width), BF16),
        ),
        in_specs=[hbm] * 11,
        out_specs=(hbm, hbm),
        scratch_shapes=[
            pltpu.VMEM((features, query_count), jnp.int32),
            pltpu.VMEM((own, features), jnp.int32),
            pltpu.VMEM((1, own), jnp.int32),
            pltpu.VMEM(bin_table.shape, BF16),
            pltpu.VMEM(rank_vector.shape, BF16),
            pltpu.VMEM(w_query.shape, BF16),
            pltpu.VMEM(w_key.shape, BF16),
            pltpu.VMEM(w_value.shape, BF16),
            pltpu.VMEM(w_out.shape, BF16),
            pltpu.VMEM(w_up.shape, BF16),
            pltpu.VMEM(w_down.shape, BF16),
            pltpu.SemaphoreType.DMA((11,)),
            pltpu.SemaphoreType.DMA((row_count // tile + 1,)),
            pltpu.VMEM((row_count, width), BF16),
            pltpu.VMEM((row_count, width), F32),
            pltpu.VMEM((row_count, width), BF16),
            pltpu.VMEM((chunks, pairs, LANES, 2 * hist_tile), BF16),
            pltpu.VMEM((chunks, pairs, 2 * hist_tile, 2 * LANES), BF16),
            pltpu.VMEM((own, LANES), F32),
            pltpu.VMEM((own, LANES), BF16),
            pltpu.VMEM((count, own, LANES), BF16),
            pltpu.VMEM((total, width), F32),
            pltpu.VMEM((total, width), BF16),
            pltpu.SemaphoreType.DMA((count,)),
            pltpu.SemaphoreType.DMA((count,)),
        ],
        compiler_params=pltpu.CompilerParams(
            collective_id=0, has_side_effects=True, vmem_limit_bytes=VMEM_LIMIT
        ),
        name="layer_rows",
    )(
        query_bins.T,
        hist_bins,
        hist_ranks.reshape(1, own),
        bin_table,
        rank_vector,
        w_query,
        w_key,
        w_value,
        w_out,
        w_up,
        w_down,
    )


def solution(mesh):
    inner = mesh.shape["qry"]
    split = P(("ctx", "qry"), None)
    return jax.shard_map(
        functools.partial(local, inner, mesh.shape["ctx"] * inner),
        mesh=mesh,
        in_specs=(split, P(("ctx", "qry")), split) + (P(),) * 8,
        out_specs=(split, split),
        check_vma=False,
    )
```

```python
import functools
import math

import jax
import jax.numpy as jnp
from jax import lax
from jax.experimental import pallas as pl
from jax.experimental.pallas import tpu as pltpu
from jax.sharding import PartitionSpec as P

HEADS = 8
LANES = 128
RADIX = 64
VMEM_LIMIT = 64 << 20
PIECES = 8
epsilon = 1e-05
F32 = jnp.float32
BF16 = jnp.bfloat16


def normalize(values):
    centered = values - jnp.mean(values, axis=-1, keepdims=True)
    variance = jnp.mean(centered * centered, axis=-1, keepdims=True)
    return centered * lax.rsqrt(variance + epsilon)


def dot(a, b):
    return jnp.dot(a, b, preferred_element_type=F32)


def embed(named, column_bin, table):
    one_hot = jnp.where(named == column_bin, 1.0, 0.0).astype(BF16)
    return dot(one_hot, table)


def layer_kernel(
    sizes,
    query_bins_hbm,
    hist_bins_hbm,
    hist_ranks_hbm,
    table_hbm,
    rank_vector_hbm,
    w_query_hbm,
    w_key_hbm,
    w_value_hbm,
    w_out_hbm,
    w_up_hbm,
    w_down_hbm,
    gathered,
    query_bins,
    hist_bins,
    hist_ranks,
    table,
    rank_vector,
    w_query,
    w_key,
    w_value,
    w_out,
    w_up,
    w_down,
    fetch_sem,
    store_sem,
    results,
    rows_out,
    queries_out,
    key_pairs,
    value_pairs,
    staged,
    mine,
    blocks,
    hist_rows,
    hist_normed,
    send_sem,
    recv_sem,
):
    inner, count, query_tile, hist_tile, tile = sizes
    own, features = hist_bins.shape
    query_count = query_bins.shape[1]
    total = count * own
    fetches = [
        pltpu.make_async_copy(source, target, fetch_sem.at[index])
        for index, (source, target) in enumerate(
            (
                (hist_bins_hbm, hist_bins),
                (hist_ranks_hbm, hist_ranks),
                (query_bins_hbm, query_bins),
                (table_hbm, table),
                (w_query_hbm, w_query),
                (rank_vector_hbm, rank_vector),
                (w_key_hbm, w_key),
                (w_value_hbm, w_value),
                (w_out_hbm, w_out),
                (w_up_hbm, w_up),
                (w_down_hbm, w_down),
            )
        )
    ]
    for fetch in fetches:
        fetch.start()
    me = lax.axis_index("ctx") * inner + lax.axis_index("qry")

    def place(index):
        return {"ctx": index // inner, "qry": index % inner}

    def partner(step):
        return (me + step) % count

    barrier = pltpu.get_barrier_semaphore()

    def greet(step, carry):
        pl.semaphore_signal(
            barrier,
            inc=1,
            device_id=place(partner(step)),
            device_id_type=pl.DeviceIdType.MESH,
        )
        return carry

    lax.fori_loop(1, count, greet, 0)

    fetches[0].wait()
    fetches[1].wait()
    ranks = jnp.broadcast_to(hist_ranks[...], (own, own))
    diagonal = lax.broadcasted_iota(jnp.int32, (own, own), 0) == lax.broadcasted_iota(
        jnp.int32, (own, own), 1
    )
    rank = jnp.sum(jnp.where(diagonal, ranks.astype(F32), 0.0), axis=1, keepdims=True)
    high = jnp.floor(rank * (1.0 / RADIX))
    staged[...] = jnp.zeros_like(staged)
    staged[:, :features] = hist_bins[...].astype(F32)
    staged[:, features : features + 1] = high
    staged[:, features + 1 : features + 2] = rank - high * RADIX
    mine[...] = staged[...].astype(BF16)
    blocks[me] = mine[...]

    bin_count = table.shape[0] // features
    wide = (features, table.shape[0])
    spread = jnp.where(
        lax.broadcasted_iota(jnp.int32, wide, 1) // bin_count
        == lax.broadcasted_iota(jnp.int32, wide, 0),
        1.0,
        0.0,
    ).astype(BF16)
    column_bin = (
        lax.broadcasted_iota(jnp.int32, (1, table.shape[0]), 1) % bin_count
    ).astype(F32)

    def copy_to(step):
        other = partner(step)
        return pltpu.make_async_remote_copy(
            src_ref=mine,
            dst_ref=blocks.at[me],
            send_sem=send_sem.at[other],
            recv_sem=recv_sem.at[me],
            device_id=place(other),
            device_id_type=pl.DeviceIdType.MESH,
        )

    def copy_from(step):
        other = partner(step)
        return pltpu.make_async_remote_copy(
            src_ref=mine,
            dst_ref=blocks.at[other],
            send_sem=send_sem.at[other],
            recv_sem=recv_sem.at[other],
            device_id=place(other),
            device_id_type=pl.DeviceIdType.MESH,
        )

    def send(step, carry):
        copy_to(step).start()
        return carry

    pl.semaphore_wait(barrier, count - 1)
    lax.fori_loop(1, count, send, 0)

    for fetch in fetches[2:5]:
        fetch.wait()

    def query_step(index, carry):
        at = pl.ds(pl.multiple_of(index * query_tile, query_tile), query_tile)
        named = lax.dot_general(
            query_bins[:, at].astype(F32).astype(BF16),
            spread,
            (((0,), (0,)), ((), ())),
            preferred_element_type=F32,
        )
        found = embed(named, column_bin, table[...])
        rows_out[at, :] = found
        queries_out[at, :] = dot(normalize(found).astype(BF16), w_query[...]).astype(BF16)
        return carry

    lax.fori_loop(0, query_count // query_tile, query_step, 0)

    def finish(step, carry):
        copy_to(step).wait_send()
        copy_from(step).wait_recv()
        return carry

    for fetch in fetches[5:8]:
        fetch.wait()
    lax.fori_loop(1, count, finish, 0)

    width = table.shape[1]
    head_dim = width // HEADS
    pairs = HEADS // 2
    left = lax.broadcasted_iota(jnp.int32, (hist_tile, LANES), 1) < head_dim
    upper = lax.broadcasted_iota(jnp.int32, (LANES, hist_tile), 0) < head_dim

    def hist_step(index, carry):
        tile_blocks = hist_tile // own
        block = blocks[pl.ds(index * tile_blocks, tile_blocks)].reshape(hist_tile, LANES)
        at = pl.ds(pl.multiple_of(index * hist_tile, hist_tile), hist_tile)
        wide_block = block.astype(F32)
        rank = (
            wide_block[:, features : features + 1] * RADIX
            + wide_block[:, features + 1 : features + 2]
        )
        level = (2.0 * rank + 1.0) / float(total) - 1.0
        found = embed(dot(block[:, :features], spread), column_bin, table[...])
        found = found + level * rank_vector[...].astype(F32).reshape(1, -1)
        hist_rows[at, :] = found
        normed = normalize(found).astype(BF16)
        hist_normed[at, :] = normed
        keys = dot(normed, w_key[...]).T
        values = dot(normed, w_value[...])
        for pair in range(pairs):
            span = slice(pair * LANES, (pair + 1) * LANES)
            key = keys[span, :]
            key_pairs[index, pair, :, :hist_tile] = jnp.where(upper, key, 0.0).astype(BF16)
            key_pairs[index, pair, :, hist_tile:] = jnp.where(upper, 0.0, key).astype(BF16)
            value = values[:, span]
            for half, keep in ((0, left), (1, jnp.logical_not(left))):
                part = slice(half * hist_tile, (half + 1) * hist_tile)
                value_pairs[index, pair, part, :LANES] = jnp.where(keep, value, 0.0).astype(BF16)
                value_pairs[index, pair, part, LANES:] = jnp.where(keep, 1.0, 0.0).astype(BF16)
        return carry

    lax.fori_loop(0, total // hist_tile, hist_step, 0)
    at = pl.ds(pl.multiple_of(me * own, own), own)
    rows_out[query_count:, :] = hist_rows[at, :]
    queries_out[query_count:, :] = dot(hist_normed[at, :], w_query[...]).astype(BF16)

    factor = math.log2(math.e) * head_dim ** (-0.5)
    chunks = total // hist_tile
    tiles = (query_count + own) // tile
    for fetch in fetches[8:]:
        fetch.wait()

    def pair_scores(at, chunk, pair):
        scores = dot(queries_out[at, pair * LANES : (pair + 1) * LANES], key_pairs[chunk, pair])
        return scores[:, :hist_tile], scores[:, hist_tile:]

    def weigh(scores, peak):
        return jnp.exp2((scores - peak) * factor).astype(BF16)

    def attend(at, pair):
        even, odd = pair_scores(at, 0, pair)
        peaks = [jnp.max(even, axis=1, keepdims=True), jnp.max(odd, axis=1, keepdims=True)]
        weights = jnp.concatenate([weigh(even, peaks[0]), weigh(odd, peaks[1])], axis=1)
        summed = dot(weights, value_pairs[0, pair])
        if chunks > 1:

            def absorb(chunk, carry):
                peak_even, peak_odd, summed = carry
                even, odd = pair_scores(at, chunk, pair)
                new_even = jnp.maximum(peak_even, jnp.max(even, axis=1, keepdims=True))
                new_odd = jnp.maximum(peak_odd, jnp.max(odd, axis=1, keepdims=True))
                weights = jnp.concatenate([weigh(even, new_even), weigh(odd, new_odd)], axis=1)
                lane = lax.broadcasted_iota(jnp.int32, summed.shape, 1) % LANES
                fade = jnp.where(
                    lane < head_dim,
                    jnp.exp2((peak_even - new_even) * factor),
                    jnp.exp2((peak_odd - new_odd) * factor),
                )
                summed = summed * fade + dot(weights, value_pairs[chunk, pair])
                return (new_even, new_odd, summed)

            summed = lax.fori_loop(1, chunks, absorb, (peaks[0], peaks[1], summed))[2]
        return (summed[:, :LANES] / summed[:, LANES:]).astype(BF16)

    def project(at, attended):
        after = rows_out[at, :] + dot(jnp.concatenate(attended, axis=1), w_out[...])
        rows_out[at, :] = after
        queries_out[at, :] = normalize(after).astype(BF16)

    ff_tile = w_up.shape[1] // pairs

    def feed(normed, part):
        span = slice(part * ff_tile, (part + 1) * ff_tile)
        hidden = jax.nn.gelu(dot(normed, w_up[:, span]), approximate=True).astype(BF16)
        return dot(hidden, w_down[span, :])

    def rows_at(index):
        return pl.ds(pl.multiple_of(index * tile, tile), tile)

    def store(index):
        at = rows_at(index)
        return pltpu.make_async_copy(results.at[at], gathered.at[at], store_sem.at[index])

    first = slice(0, tile)
    project(first, [attend(first, pair) for pair in range(pairs)])

    def tile_step(index, carry):
        at, before = rows_at(index), rows_at(index - 1)
        normed = queries_out[before, :]
        result = rows_out[before, :]
        attended = []
        for pair in range(pairs):
            attended.append(attend(at, pair))
            if pair < pairs - 1:
                result = result + feed(normed, pair)
        project(at, attended)
        results[before, :] = (result + feed(normed, pairs - 1)).astype(BF16)
        store(index - 1).start()
        return carry

    lax.fori_loop(1, tiles, tile_step, 0)
    start = (tiles - 1) * tile
    normed = queries_out[start:, :]
    result = rows_out[start:, :]
    for part in range(pairs):
        result = result + feed(normed, part)
    result = result.astype(BF16)
    results[start:, :] = result
    store(tiles - 1).start()
    for index in range(tiles):
        store(index).wait()


def hand_out_kernel(results, hist_out, query_out, held, load_sem, store_sem):
    query_count = query_out.shape[0]
    piece = query_count // PIECES
    loads, stores = [], []
    for index in range(PIECES + 1):
        at = slice(index * piece, (index + 1) * piece if index < PIECES else held.shape[0])
        target = query_out.at[at] if index < PIECES else hist_out
        loads.append(pltpu.make_async_copy(results.at[at], held.at[at], load_sem.at[index]))
        stores.append(pltpu.make_async_copy(held.at[at], target, store_sem.at[index]))
    for load in loads:
        load.start()
    for load, store in zip(loads, stores):
        load.wait()
        store.start()
    for store in stores:
        store.wait()


def local(
    inner,
    count,
    hist_bins,
    hist_ranks,
    query_bins,
    bin_table,
    rank_vector,
    w_query,
    w_key,
    w_value,
    w_out,
    w_up,
    w_down,
):
    own = hist_bins.shape[0]
    query_count = query_bins.shape[0]
    width = bin_table.shape[1]
    total = own * count
    row_count = own + query_count
    hist_tile = math.gcd(total, 512)
    query_tile = math.gcd(query_count, 256)
    chunks = total // hist_tile
    features = hist_bins.shape[1]
    pairs = HEADS // 2
    tile = max(
        size for size in range(16, 257, 16) if row_count % size == 0 and size > own
    )
    hbm = pl.BlockSpec(memory_space=pltpu.HBM)
    results = pl.pallas_call(
        functools.partial(
            layer_kernel,
            (inner, count, query_tile, hist_tile, tile),
        ),
        out_shape=jax.ShapeDtypeStruct((row_count, width), BF16),
        in_specs=[hbm] * 11,
        out_specs=hbm,
        scratch_shapes=[
            pltpu.VMEM((features, query_count), jnp.int32),
            pltpu.VMEM((own, features), jnp.int32),
            pltpu.VMEM((1, own), jnp.int32),
            pltpu.VMEM(bin_table.shape, BF16),
            pltpu.VMEM(rank_vector.shape, BF16),
            pltpu.VMEM(w_query.shape, BF16),
            pltpu.VMEM(w_key.shape, BF16),
            pltpu.VMEM(w_value.shape, BF16),
            pltpu.VMEM(w_out.shape, BF16),
            pltpu.VMEM(w_up.shape, BF16),
            pltpu.VMEM(w_down.shape, BF16),
            pltpu.SemaphoreType.DMA((11,)),
            pltpu.SemaphoreType.DMA((row_count // tile + 1,)),
            pltpu.VMEM((row_count, width), BF16),
            pltpu.VMEM((row_count, width), F32),
            pltpu.VMEM((row_count, width), BF16),
            pltpu.VMEM((chunks, pairs, LANES, 2 * hist_tile), BF16),
            pltpu.VMEM((chunks, pairs, 2 * hist_tile, 2 * LANES), BF16),
            pltpu.VMEM((own, LANES), F32),
            pltpu.VMEM((own, LANES), BF16),
            pltpu.VMEM((count, own, LANES), BF16),
            pltpu.VMEM((total, width), F32),
            pltpu.VMEM((total, width), BF16),
            pltpu.SemaphoreType.DMA((count,)),
            pltpu.SemaphoreType.DMA((count,)),
        ],
        compiler_params=pltpu.CompilerParams(
            collective_id=0, has_side_effects=True, vmem_limit_bytes=VMEM_LIMIT
        ),
        name="layer_rows",
    )(
        query_bins.T,
        hist_bins,
        hist_ranks.reshape(1, own),
        bin_table,
        rank_vector,
        w_query,
        w_key,
        w_value,
        w_out,
        w_up,
        w_down,
    )
    return pl.pallas_call(
        hand_out_kernel,
        out_shape=(
            jax.ShapeDtypeStruct((own, width), BF16),
            jax.ShapeDtypeStruct((query_count, width), BF16),
        ),
        in_specs=[hbm],
        out_specs=(hbm, hbm),
        scratch_shapes=[
            pltpu.VMEM((row_count, width), BF16),
            pltpu.SemaphoreType.DMA((PIECES + 1,)),
            pltpu.SemaphoreType.DMA((PIECES + 1,)),
        ],
        compiler_params=pltpu.CompilerParams(vmem_limit_bytes=VMEM_LIMIT),
        name="hand_out",
    )(results)


def solution(mesh):
    inner = mesh.shape["qry"]
    split = P(("ctx", "qry"), None)
    return jax.shard_map(
        functools.partial(local, inner, mesh.shape["ctx"] * inner),
        mesh=mesh,
        in_specs=(split, P(("ctx", "qry")), split) + (P(),) * 8,
        out_specs=(split, split),
        check_vma=False,
    )
```
